32 devices in a mesh: group: 2 (over y), patch: 4 (over z), section: 4 (over x, core).
Axes of the slice: x: 2, y: 2, z: 4, core: 2. Of those that a mesh axis runs over, the one named last changes fastest.
Arguments:
- hidden: bfloat16 [4, 8, 2560], P('section', 'patch'), may hold values from -6 to 6
- kv_cache: bfloat16 [4, 64, 2, 2560], P('section', ('group', 'patch')), parts along dimension 1, may hold values from -7 to 7
- step_index: int32 [8], P('group'), parts along dimension 0, may hold values from 0 to 14
- mod_table: float32 [16, 4, 3, 2560], P(None, 'section'), may hold values from -4 to 4
- query_gain: float32 [4, 2560], P('section'), may hold values from -6 to 6
- key_gain: float32 [4, 2560], P('section'), may hold values from -6 to 6
Outputs:
- hidden_out: bfloat16 [4, 16, 2560], P('section', ('group', 'patch')), parts along dimension 1
- cache_out: bfloat16 [4, 64, 2, 2560], P('section', ('group', 'patch')), parts along dimension 1
The draws below stay inside these ranges and needn't reach their ends.
There are 2 independent parts, one for each index of `group`. The reference program is written for one: setup_inputs(seed, part) draws one part's arguments, and reference() takes and returns one part's arrays. A program takes and returns all parts, laid end to end along the dimension named above; an argument that names none is the same for every part. Nothing has to cross between parts.
All inputs are finite; a program needn't handle non-finite values.
Results may differ from the reference program's by a relative error of at most 0.025.
Values may be sent and summed in bfloat16 or wider, within the bound.
No kernel may reach another device: no remote copies, remote signals or barrier semaphores. Data moves between devices by JAX's collectives and lax.ppermute only.
A program may use at most 64 MiB of HBM per device.

```python
import jax
import jax.numpy as jnp
from jax import lax

HEAD = 128
HEADS = 20
C = 2560
MB = 2
STEPS = 16
TICKS = 4
LAYERS = 4
MICRO = 4
TOKENS = 32
N_PATCH = 4


def touch_ends(array, key, smallest, largest):
    dims = array.shape
    index_at = [jax.random.randint(jax.random.fold_in(key, axis), (), 0, dims[axis]) for axis in range(len(dims))]
    array = array.at[tuple(index_at)].set(smallest)
    longest = dims.index(max(dims))
    index_at[longest] = (index_at[longest] + 1) % dims[longest]
    return array.at[tuple(index_at)].set(largest)


def level_of(own_key, extent, shards, smallest, high):
    level, own = 1.0, jax.random.fold_in(own_key, 6)
    for dim, blocks in shards:
        steps = jnp.exp(jax.random.uniform(jax.random.fold_in(own, dim), (blocks,), jnp.float32, smallest / len(shards), high / len(shards)))
        level = level * jnp.repeat(steps, extent[dim] // blocks).reshape([-1 if axis == dim else 1 for axis in range(len(extent))])
    return level


def bell_draw(key, dims, deviation, reach, pieces=(), dtype=jnp.bfloat16):
    factor_of = level_of(key, dims, pieces, -0.22, 0.18) if pieces else 1.0
    array = jax.random.normal(key, dims, jnp.float32) * deviation * factor_of
    return jnp.minimum(jnp.maximum(array, -reach), reach).astype(dtype)


def setup_inputs(seed: int = 0, part: int = 0) -> dict:
    key_of = jax.random.split(jax.random.key(seed), 7)
    part_splits = jax.random.split(jax.random.fold_in(key_of[6], part), 7)
    return {
        "hidden": bell_draw(key_of[0], (MICRO, N_PATCH * MB, C), 1.0, 6.0, ((0, 4), (1, 4))),
        "kv_cache": bell_draw(part_splits[1], (LAYERS, TOKENS, 2, C), 1.2, 7.0, ((0, 4), (1, 4))),
        "step_index": touch_ends(jax.random.randint(part_splits[2], (MICRO,), 0, STEPS - 1), jax.random.fold_in(part_splits[2], 1), 0, (STEPS - 1) - 1).astype(jnp.int32),
        "mod_table": bell_draw(key_of[3], (STEPS, LAYERS, 3, C), 0.8, 4.0, ((1, 4),), jnp.float32),
        "query_gain": bell_draw(key_of[4], (LAYERS, C), 1.4, 6.0, ((0, 4),), jnp.float32),
        "key_gain": bell_draw(key_of[5], (LAYERS, C), 1.4, 6.0, ((0, 4),), jnp.float32),
    }


def modulate(rows_in, shift_row, scale_row):
    average = lax.optimization_barrier(jnp.mean(rows_in, axis=-1, keepdims=True))
    centred = rows_in - average
    variance = lax.optimization_barrier(jnp.mean(centred * centred, axis=-1, keepdims=True))
    return centred / jnp.sqrt(variance + 1e-06) * (1.0 + scale_row) + shift_row

def head_norm(rows_in):
    shaped = rows_in.reshape(rows_in.shape[0], HEADS, HEAD)
    square = lax.optimization_barrier(jnp.mean(shaped * shaped, axis=-1, keepdims=True))
    return (shaped / jnp.sqrt(square + 1e-06)).reshape(rows_in.shape)

def attend(queries, keys_all, values_all):
    count = queries.shape[0]
    query_heads = queries.astype(jnp.float32).reshape(count, HEADS, HEAD)
    key_heads = keys_all.astype(jnp.float32).reshape(-1, HEADS, HEAD)
    value_heads = values_all.astype(jnp.float32).reshape(-1, HEADS, HEAD)
    scores = jnp.einsum('rhd,khd->rhk', query_heads, key_heads) * HEAD ** (-0.5)
    highest = lax.optimization_barrier(jnp.max(scores, axis=-1, keepdims=True))
    weights = jnp.exp(scores - highest).astype(jnp.bfloat16).astype(jnp.float32)
    totals = lax.optimization_barrier(jnp.sum(weights, axis=-1))
    summed = jnp.einsum('rhk,khd->rhd', weights, value_heads)
    return (summed / totals[:, :, None]).reshape(count, HEADS * HEAD)

def reference(hidden, kv_cache, step_index, mod_table, query_gain, key_gain):
    sections = hidden.shape[0]
    width = hidden.shape[2]
    cache = kv_cache.reshape(sections, N_PATCH, sections, MB, 2, width)
    states = [hidden[index] for index in range(sections)]
    for tick_num in range(TICKS):
        for micro in range(sections):
            layer = (micro + tick_num) % sections
            wraps = (micro + tick_num) // sections
            stamp = step_index[micro] + wraps
            picked = mod_table[stamp, layer]
            modulated = modulate(states[micro].astype(jnp.float32), picked[0], picked[1])
            normed = head_norm(modulated)
            queries = (normed * query_gain[layer]).astype(jnp.bfloat16)
            keys_now = (normed * key_gain[layer]).astype(jnp.bfloat16)
            values_now = modulated.astype(jnp.bfloat16)
            fresh = jnp.stack([keys_now, values_now], axis=1).reshape(N_PATCH, 1, MB, 2, width)
            layer_cache = cache[layer].at[:, micro:micro + 1].set(fresh)
            cache = cache.at[layer].set(layer_cache)
            flat = layer_cache.reshape(-1, 2, width)
            attended = attend(queries, flat[:, 0], flat[:, 1])
            states[micro] = (states[micro].astype(jnp.float32) + picked[2] * attended).astype(jnp.bfloat16)
    result = jnp.stack([states[(index - TICKS) % sections] for index in range(sections)])
    return (result, cache.reshape(kv_cache.shape))
```

```python
import jax
import jax.numpy as jnp
from jax import lax
from jax.experimental import pallas as pl
from jax.experimental.pallas import tpu as pltpu
from jax.sharding import PartitionSpec as P

HEAD = 128
HEADS = 20
TICKS = 4
ROWS = 8
STALE = 32
SLOTS = STALE + TICKS * ROWS


def from_behind(value, axis, steps):
    count = lax.axis_size(axis)
    pairs = [(source, (source + steps) % count) for source in range(count)]
    return lax.ppermute(value, axis, pairs)


def modulate(rows_in, shift_row, scale_row):
    average = jnp.mean(rows_in, axis=-1, keepdims=True)
    centred = rows_in - average
    variance = jnp.mean(centred * centred, axis=-1, keepdims=True)
    return centred / jnp.sqrt(variance + 1e-06) * (1.0 + scale_row) + shift_row


def head_norm(rows_in):
    shaped = rows_in.reshape(rows_in.shape[0], HEADS, HEAD)
    square = jnp.mean(shaped * shaped, axis=-1, keepdims=True)
    return (shaped / jnp.sqrt(square + 1e-06)).reshape(rows_in.shape)


def attend(queries, keys_all, values_all):
    count = queries.shape[0]
    query_heads = queries.reshape(count, HEADS, HEAD)
    key_heads = keys_all.reshape(-1, HEADS, HEAD)
    value_heads = values_all.reshape(-1, HEADS, HEAD)
    scores = jnp.einsum(
        "rhd,khd->rhk", query_heads, key_heads, preferred_element_type=jnp.float32
    ) * HEAD ** (-0.5)
    highest = jnp.max(scores, axis=-1)
    weights = jnp.exp(scores - highest[:, :, None]).astype(jnp.bfloat16)
    totals = jnp.sum(weights.astype(jnp.float32), axis=-1)
    summed = jnp.einsum("rhk,khd->rhd", weights, value_heads, preferred_element_type=jnp.float32)
    return (summed / totals[:, :, None]).reshape(count, HEADS * HEAD)


def general_shards(hidden, kv_cache, step_index, mod_table, query_gain, key_gain):
    sections = lax.axis_size("section")
    patches = lax.axis_size("patch")
    section_now = lax.axis_index("section")
    state = hidden[0]
    rows = state.shape[0]
    width = state.shape[1]
    own_cache = kv_cache[0].reshape(sections, rows, 2, width)
    table = mod_table[:, 0]
    whole = lax.all_gather(kv_cache[0], "patch", axis=0, tiled=True).reshape(
        patches, sections, rows, 2, width
    )
    for tick_num in range(TICKS):
        micro = (section_now - tick_num) % sections
        wraps = (micro + tick_num) // sections
        stamp = jnp.sum(jnp.where(jnp.arange(sections) == micro, step_index, 0)) + wraps
        chooser = (jnp.arange(table.shape[0]) == stamp)[:, None, None]
        picked = jnp.sum(jnp.where(chooser, table, 0.0), axis=0)
        modulated = modulate(state.astype(jnp.float32), picked[0], picked[1])
        normed = head_norm(modulated)
        queries = (normed * query_gain[0]).astype(jnp.bfloat16)
        keys_now = (normed * key_gain[0]).astype(jnp.bfloat16)
        fresh = jnp.stack([keys_now, modulated.astype(jnp.bfloat16)], axis=1)
        own_cache = lax.dynamic_update_slice_in_dim(own_cache, fresh[None], micro, 0)
        fresh_all = lax.all_gather(fresh, "patch", axis=0, tiled=True).reshape(
            patches, 1, rows, 2, width
        )
        whole = lax.dynamic_update_slice_in_dim(whole, fresh_all, micro, 1)
        flat = whole.reshape(-1, 2, width)
        attended = attend(queries, flat[:, 0], flat[:, 1])
        updated = (state.astype(jnp.float32) + picked[2] * attended).astype(jnp.bfloat16)
        state = from_behind(updated, "section", 1)
    return (state[None], own_cache.reshape(kv_cache.shape))


def swap(value, axis, bit):
    count = lax.axis_size(axis)
    return lax.ppermute(value, axis, [(source, source ^ bit) for source in range(count)])


def project(rows_in, mods, layer, tick):
    shift_row = mods[layer, 3 * tick]
    scale_row = mods[layer, 3 * tick + 1]
    average = jnp.mean(rows_in, axis=-1, keepdims=True)
    centred = rows_in - average
    variance = jnp.mean(centred * centred, axis=-1, keepdims=True)
    modulated = centred * lax.rsqrt(variance + 1e-06) * (1.0 + scale_row) + shift_row
    normed = []
    for head in range(HEADS):
        part = modulated[:, head * HEAD : (head + 1) * HEAD]
        square = jnp.mean(part * part, axis=-1, keepdims=True)
        normed.append(part * lax.rsqrt(square + 1e-06))
    normed = jnp.concatenate(normed, axis=1)
    queries = (normed * mods[layer, 3 * TICKS]).astype(jnp.bfloat16)
    keys_now = (normed * mods[layer, 3 * TICKS + 1]).astype(jnp.bfloat16)
    return queries, keys_now, modulated.astype(jnp.bfloat16)


def refresh(keys, values, layer, tick, keys_now, values_now):
    place = STALE + tick * ROWS
    keys[layer, place : place + ROWS] = keys_now
    values[layer, place : place + ROWS] = values_now


def valid_keys(rows, tick):
    lane = lax.broadcasted_iota(jnp.int32, (rows, SLOTS), 1)
    stale = (lane < STALE) & (lane % 8 < 2 * (TICKS - 1 - tick))
    fresh = (lane >= STALE) & (lane < STALE + (tick + 1) * ROWS)
    return stale | fresh


def attended_rows(queries, keys, values, layer, valid):
    parts = []
    for head in range(HEADS):
        span = slice(head * HEAD, (head + 1) * HEAD)
        scores = lax.dot_general(
            queries[:, span],
            keys[layer, :, span],
            (((1,), (1,)), ((), ())),
            preferred_element_type=jnp.float32,
        )
        if valid is not None:
            scores = jnp.where(valid, scores, -3.0e38)
        highest = jnp.max(scores, axis=-1, keepdims=True)
        weights = jnp.exp((scores - highest) * HEAD ** (-0.5)).astype(jnp.bfloat16)
        total = jnp.sum(weights.astype(jnp.float32), axis=-1, keepdims=True)
        summed = jnp.dot(weights, values[layer, :, span], preferred_element_type=jnp.float32)
        parts.append(summed / total)
    return jnp.concatenate(parts, axis=1)


def advance(rows_in, mods, layer, tick, attended):
    gate_row = mods[layer, 3 * tick + 2]
    return (rows_in + gate_row * attended).astype(jnp.bfloat16)


def first_kernel(section, own, other, own_mods, other_mods, keys, values, mods, sent):
    @pl.when(section[0] % 2 == 0)
    def _():
        mods[0] = own_mods[...]
        mods[1] = other_mods[...]

    @pl.when(section[0] % 2 != 0)
    def _():
        mods[1] = own_mods[...]
        mods[0] = other_mods[...]

    def fill(layer, chunks):
        for index, chunk in enumerate(chunks):
            keys[layer, index * 8 : index * 8 + 8] = chunk[0:8]
            values[layer, index * 8 : index * 8 + 8] = chunk[8:16]
        keys[layer, STALE:] = jnp.zeros((SLOTS - STALE, keys.shape[2]), keys.dtype)
        values[layer, STALE:] = jnp.zeros((SLOTS - STALE, keys.shape[2]), keys.dtype)

    @pl.when(section[0] % 2 == 0)
    def _():
        fill(0, own)
        fill(1, other)

    @pl.when(section[0] % 2 != 0)
    def _():
        fill(1, own)
        fill(0, other)

    def entering(layer):
        parts = [keys[layer, index * 8 + 6 : index * 8 + 8].astype(jnp.float32) for index in range(4)]
        return jnp.concatenate(parts, axis=0)

    valid = valid_keys(ROWS, 0)
    after = []
    for layer in range(2):
        rows_in = entering(layer)
        queries, keys_now, values_now = project(rows_in, mods, layer, 0)
        refresh(keys, values, layer, 0, keys_now, values_now)
        attended = attended_rows(queries, keys, values, layer, valid)
        after.append(advance(rows_in, mods, layer, 0, attended))
    rows_in = after[0].astype(jnp.float32)
    queries, keys_now, values_now = project(rows_in, mods, 1, 1)
    refresh(keys, values, 1, 1, keys_now, values_now)
    attended = attended_rows(queries, keys, values, 1, valid_keys(ROWS, 1))
    sent[0:ROWS] = advance(rows_in, mods, 1, 1, attended)
    sent[ROWS:] = after[1]


def second_kernel(came, mods, keys_in, values_in, keys, values, sent):
    keys[...] = keys_in[...]
    values[...] = values_in[...]
    third = came[0:ROWS].astype(jnp.float32)
    fourth = came[ROWS:].astype(jnp.float32)
    for layer, low in ((0, 1), (1, 2)):
        queries_d, keys_now, values_now = project(fourth, mods, layer, low)
        refresh(keys, values, layer, low, keys_now, values_now)
        queries_c, keys_now, values_now = project(third, mods, layer, low + 1)
        refresh(keys, values, layer, low + 1, keys_now, values_now)
        queries = jnp.concatenate([queries_c, queries_d], axis=0)
        valid = jnp.concatenate(
            [valid_keys(ROWS, low + 1).astype(jnp.int32), valid_keys(ROWS, low).astype(jnp.int32)], axis=0
        ) > 0
        attended = attended_rows(queries, keys, values, layer, valid)
        third = advance(third, mods, layer, low + 1, attended[:ROWS]).astype(jnp.float32)
        fourth = advance(fourth, mods, layer, low, attended[ROWS:]).astype(jnp.float32)
    sent[0:ROWS] = third.astype(jnp.bfloat16)
    sent[ROWS:] = fourth.astype(jnp.bfloat16)


def third_kernel(section, came, mods, keys_in, values_in, hidden, cache, keys, values):
    rows_in = came[ROWS:].astype(jnp.float32)
    queries, keys_now, values_now = project(rows_in, mods, 0, 3)
    old = (TICKS - 1) * ROWS
    keys[0, 0:old] = keys_in[0, STALE : STALE + old]
    values[0, 0:old] = values_in[0, STALE : STALE + old]
    keys[0, old:] = keys_now
    values[0, old:] = values_now
    attended = attended_rows(queries, keys, values, 0, None)
    ended = advance(rows_in, mods, 0, 3, attended)

    def emit(ended_rows, layer, keys_last, values_last):
        hidden[...] = ended_rows
        for tick in range(TICKS):
            start = STALE + tick * ROWS
            micro = lax.rem(section[0] + TICKS - tick, TICKS)
            for part, source, last in ((0, keys_in, keys_last), (1, values_in, values_last)):
                rows = last if tick == TICKS - 1 and last is not None else source[layer, start : start + ROWS]
                for row in range(2):
                    cache[micro * 2 + row, part : part + 1] = rows[row : row + 1]

    @pl.when(section[0] % 2 == 0)
    def _():
        emit(came[0:2], 0, keys_now, values_now)

    @pl.when(section[0] % 2 != 0)
    def _():
        emit(ended[0:2], 1, None, None)


def pick_kernel(section, steps, table, query_gain, key_gain, out, sem):
    copies = []
    for tick in range(TICKS):
        micro = lax.rem(section[0] + TICKS - tick, TICKS)
        stamp = steps[micro] + (micro > section[0]).astype(jnp.int32)
        copies.append(pltpu.make_async_copy(table.at[stamp], out.at[pl.ds(3 * tick, 3)], sem.at[tick]))
    copies.append(pltpu.make_async_copy(query_gain, out.at[3 * TICKS], sem.at[TICKS]))
    copies.append(pltpu.make_async_copy(key_gain, out.at[3 * TICKS + 1], sem.at[TICKS + 1]))
    for copy in copies:
        copy.start()
    for copy in copies:
        copy.wait()


VMEM = pl.BlockSpec(memory_space=pltpu.VMEM)
SMEM = pl.BlockSpec(memory_space=pltpu.SMEM)
ANY = pl.BlockSpec(memory_space=pl.ANY)


def call(kernel, name, out_shape, in_specs, scratch=()):
    return pl.pallas_call(
        kernel,
        out_shape=out_shape,
        in_specs=in_specs,
        out_specs=jax.tree.map(lambda _: VMEM, out_shape),
        scratch_shapes=list(scratch),
        compiler_params=pltpu.CompilerParams(vmem_limit_bytes=8 << 20),
        name=name,
    )


def fast_shards(hidden, kv_cache, step_index, mod_table, query_gain, key_gain):
    width = hidden.shape[-1]
    section_now = lax.axis_index("section")
    section = section_now.reshape(1).astype(jnp.int32)
    shape = jax.ShapeDtypeStruct
    bf16 = jnp.bfloat16

    cached = kv_cache[0].reshape(TICKS, 2, 2, width)
    cached = jnp.concatenate([cached, cached], axis=0)
    stale = lax.dynamic_slice_in_dim(cached, section_now + 1, TICKS - 1, 0)
    stale = stale.reshape(6, 2, width)
    pack = jnp.concatenate([stale[:, 0], hidden[0], stale[:, 1], hidden[0]], axis=0)
    own = [pack] + [swap(pack, "patch", bit) for bit in (1, 2, 3)]
    other = [swap(chunk, "section", 1) for chunk in own]

    own_mods = call(
        pick_kernel,
        "pick",
        shape((3 * TICKS + 2, 1, width), jnp.float32),
        [SMEM, SMEM, ANY, ANY, ANY],
        [pltpu.SemaphoreType.DMA((TICKS + 2,))],
    )(section, step_index, mod_table.reshape(-1, 3, 1, width), query_gain, key_gain)
    other_mods = swap(own_mods, "section", 1)

    both = shape((2, SLOTS, width), bf16)

    def first(section_ref, *refs):
        first_kernel(section_ref, refs[0:4], refs[4:8], *refs[8:])

    sends = shape((2 * ROWS, width), bf16)
    mods_shape = shape((2, 3 * TICKS + 2, 1, width), jnp.float32)
    keys, values, mods, sent = call(
        first, "first", (both, both, mods_shape, sends), [SMEM] + [VMEM] * 10
    )(section, *own, *other, own_mods, other_mods)
    came = swap(sent, "section", 2)
    keys, values, sent = call(second_kernel, "second", (both, both, sends), [VMEM] * 4)(
        came, mods, keys, values
    )
    came = swap(sent, "section", 2)
    ended, cache = call(
        third_kernel,
        "third",
        (shape((2, width), bf16), shape((2 * TICKS, 2, width), bf16)),
        [SMEM] + [VMEM] * 4,
        [pltpu.VMEM((1, TICKS * ROWS, width), bf16)] * 2,
    )(section, came, mods, keys, values)
    return ended[None], cache[None]


def solution(mesh):
    in_specs = (
        P("section", "patch", None),
        P("section", ("group", "patch"), None, None),
        P("group"),
        P(None, "section", None, None),
        P("section", None),
        P("section", None),
    )
    out_specs = (
        P("section", ("group", "patch"), None),
        P("section", ("group", "patch"), None, None),
    )
    fits = mesh.shape["section"] == TICKS and mesh.shape["patch"] == 4
    shards = fast_shards if fits else general_shards
    return jax.shard_map(shards, mesh=mesh, in_specs=in_specs, out_specs=out_specs, check_vma=False)
```

```python
import jax
import jax.numpy as jnp
from jax import lax
from jax.experimental import pallas as pl
from jax.experimental.pallas import tpu as pltpu
from jax.sharding import PartitionSpec as P

HEAD = 128
HEADS = 20
TICKS = 4
ROWS = 8
STALE = 32
SLOTS = STALE + TICKS * ROWS
PIECE = 640
CHUNK = 7 * PIECE


def from_behind(value, axis, steps):
    count = lax.axis_size(axis)
    pairs = [(source, (source + steps) % count) for source in range(count)]
    return lax.ppermute(value, axis, pairs)


def modulate(rows_in, shift_row, scale_row):
    average = jnp.mean(rows_in, axis=-1, keepdims=True)
    centred = rows_in - average
    variance = jnp.mean(centred * centred, axis=-1, keepdims=True)
    return centred / jnp.sqrt(variance + 1e-06) * (1.0 + scale_row) + shift_row


def head_norm(rows_in):
    shaped = rows_in.reshape(rows_in.shape[0], HEADS, HEAD)
    square = jnp.mean(shaped * shaped, axis=-1, keepdims=True)
    return (shaped / jnp.sqrt(square + 1e-06)).reshape(rows_in.shape)


def attend(queries, keys_all, values_all):
    count = queries.shape[0]
    query_heads = queries.reshape(count, HEADS, HEAD)
    key_heads = keys_all.reshape(-1, HEADS, HEAD)
    value_heads = values_all.reshape(-1, HEADS, HEAD)
    scores = jnp.einsum(
        "rhd,khd->rhk", query_heads, key_heads, preferred_element_type=jnp.float32
    ) * HEAD ** (-0.5)
    highest = jnp.max(scores, axis=-1)
    weights = jnp.exp(scores - highest[:, :, None]).astype(jnp.bfloat16)
    totals = jnp.sum(weights.astype(jnp.float32), axis=-1)
    summed = jnp.einsum("rhk,khd->rhd", weights, value_heads, preferred_element_type=jnp.float32)
    return (summed / totals[:, :, None]).reshape(count, HEADS * HEAD)


def general_shards(hidden, kv_cache, step_index, mod_table, query_gain, key_gain):
    sections = lax.axis_size("section")
    patches = lax.axis_size("patch")
    section_now = lax.axis_index("section")
    state = hidden[0]
    rows = state.shape[0]
    width = state.shape[1]
    own_cache = kv_cache[0].reshape(sections, rows, 2, width)
    table = mod_table[:, 0]
    whole = lax.all_gather(kv_cache[0], "patch", axis=0, tiled=True).reshape(
        patches, sections, rows, 2, width
    )
    for tick_num in range(TICKS):
        micro = (section_now - tick_num) % sections
        wraps = (micro + tick_num) // sections
        stamp = jnp.sum(jnp.where(jnp.arange(sections) == micro, step_index, 0)) + wraps
        chooser = (jnp.arange(table.shape[0]) == stamp)[:, None, None]
        picked = jnp.sum(jnp.where(chooser, table, 0.0), axis=0)
        modulated = modulate(state.astype(jnp.float32), picked[0], picked[1])
        normed = head_norm(modulated)
        queries = (normed * query_gain[0]).astype(jnp.bfloat16)
        keys_now = (normed * key_gain[0]).astype(jnp.bfloat16)
        fresh = jnp.stack([keys_now, modulated.astype(jnp.bfloat16)], axis=1)
        own_cache = lax.dynamic_update_slice_in_dim(own_cache, fresh[None], micro, 0)
        fresh_all = lax.all_gather(fresh, "patch", axis=0, tiled=True).reshape(
            patches, 1, rows, 2, width
        )
        whole = lax.dynamic_update_slice_in_dim(whole, fresh_all, micro, 1)
        flat = whole.reshape(-1, 2, width)
        attended = attend(queries, flat[:, 0], flat[:, 1])
        updated = (state.astype(jnp.float32) + picked[2] * attended).astype(jnp.bfloat16)
        state = from_behind(updated, "section", 1)
    return (state[None], own_cache.reshape(kv_cache.shape))


def swap(value, axis, bit):
    count = lax.axis_size(axis)
    return lax.ppermute(value, axis, [(source, source ^ bit) for source in range(count)])


def mod_row(mods, index):
    return mods[pl.ds(index, ROWS, stride=0), :]


def project(rows_in, mods, tick):
    shift_row = mod_row(mods, 3 * tick)
    scale_row = mod_row(mods, 3 * tick + 1)
    average = jnp.mean(rows_in, axis=-1, keepdims=True)
    centred = rows_in - average
    variance = jnp.mean(centred * centred, axis=-1, keepdims=True)
    modulated = centred * lax.rsqrt(variance + 1e-06) * (1.0 + scale_row) + shift_row
    normed = []
    for head in range(HEADS):
        part = modulated[:, head * HEAD : (head + 1) * HEAD]
        square = jnp.mean(part * part, axis=-1, keepdims=True)
        normed.append(part * lax.rsqrt(square + 1e-06))
    return modulated, jnp.concatenate(normed, axis=1)


GROUPS = ((0, 8), (8, 16), (16, 20))


def clear_placed(*placed):
    for place in placed:
        place[...] = jnp.zeros_like(place)


def weigh(scores, tick):
    key = lax.broadcasted_iota(jnp.int32, scores.shape, 0)
    stale = (key < STALE) & (key % 8 < 2 * (TICKS - 1 - tick))
    fresh = (key >= STALE) & (key < STALE + (tick + 1) * ROWS)
    scores = jnp.where(stale | fresh, scores, -3.0e38)
    highest = jnp.max(scores, axis=0, keepdims=True)
    weights = jnp.exp((scores - highest) * HEAD ** (-0.5))
    return weights.T.astype(jnp.bfloat16)


def steps(group, keys, values):
    made = []
    for rows_in, mods, layer, tick, placed in group:
        modulated, normed = project(rows_in, mods, tick)
        slot = slice(STALE + tick * ROWS, STALE + (tick + 1) * ROWS)
        keys[layer, slot] = (normed * mod_row(mods, 3 * TICKS + 1)).astype(jnp.bfloat16)
        values[layer, slot] = modulated.astype(jnp.bfloat16)
        if placed is not None:
            made.append((normed * mod_row(mods, 3 * TICKS)).astype(jnp.bfloat16))
    group = [entry for entry in group if entry[4] is not None]
    for queries, (_, _, _, _, placed) in zip(made, group):
        for place, (begin, end) in zip(placed, GROUPS):
            for head in range(begin, end):
                low = head - begin
                place[low * ROWS : (low + 1) * ROWS, low * HEAD : (low + 1) * HEAD] = queries[
                    :, head * HEAD : (head + 1) * HEAD
                ]
    against = (((1,), (1,)), ((), ()))
    scores = [
        [
            lax.dot_general(
                keys[layer, :, begin * HEAD : end * HEAD],
                place[...],
                against,
                preferred_element_type=jnp.float32,
            )
            for place, (begin, end) in zip(placed, GROUPS)
        ]
        for _, _, layer, _, placed in group
    ]
    weights = [
        [weigh(part, entry[3]) for part in parts] for parts, entry in zip(scores, group)
    ]
    ones = jnp.ones((SLOTS, HEAD), jnp.bfloat16)
    results = []
    for chosen, (rows_in, mods, layer, tick, _) in zip(weights, group):
        parts = []
        for part, (begin, end) in zip(chosen, GROUPS):
            totals = jnp.dot(part, ones, preferred_element_type=jnp.float32)
            for head in range(begin, end, 2):
                low = (head - begin) * ROWS
                summed = jnp.dot(
                    part[low : low + 2 * ROWS],
                    values[layer, :, head * HEAD : (head + 2) * HEAD],
                    preferred_element_type=jnp.float32,
                )
                parts.append(summed[0:ROWS, 0:HEAD] / totals[low : low + ROWS])
                parts.append(summed[ROWS:, HEAD:] / totals[low + ROWS : low + 2 * ROWS])
        attended = jnp.concatenate(parts, axis=1)
        results.append((rows_in + mod_row(mods, 3 * tick + 2) * attended).astype(jnp.bfloat16))
    return results


def fill(layers, keys, values, states):
    width = keys.shape[2]
    pieces = width // PIECE

    @pl.loop(0, pieces)
    def _(index):
        span = pl.ds(pl.multiple_of(index * PIECE, PIECE), PIECE)
        beside = pl.ds(pl.multiple_of(width + jnp.minimum(index, pieces - 2) * PIECE, PIECE), PIECE)
        for layer, chunks in layers:
            entering = []
            for number, chunk in enumerate(chunks):
                keys[layer, number * 8 : number * 8 + 8, span] = chunk[:, span]
                values[layer, number * 8 : number * 8 + 8, span] = chunk[:, beside]
                entering.append(chunk[6:8, span].astype(jnp.float32))
            states[layer, :, span] = jnp.concatenate(entering, axis=0).astype(jnp.bfloat16)
            values[layer, STALE:, span] = jnp.zeros((SLOTS - STALE, PIECE), values.dtype)

    last = width - PIECE
    for layer, chunks in layers:
        for number, chunk in enumerate(chunks):
            for pair in range(3):
                low = number * 8 + 2 * pair
                beside = width + pair * PIECE
                values[layer, low : low + 2, last:] = chunk[6:8, beside : beside + PIECE]


def load_kernel(
    section, steps, cache, hidden, table, query_gain, key_gain, out, out_mods, stale, entering, rows, sem
):
    copies = [pltpu.make_async_copy(hidden.at[0], entering, sem.at[0])]
    for later in range(1, TICKS):
        micro = lax.rem(section[0] + later, TICKS)
        copies.append(
            pltpu.make_async_copy(
                cache.at[0, pl.ds(2 * micro, 2)], stale.at[pl.ds(2 * later - 2, 2)], sem.at[later]
            )
        )
    for tick in range(TICKS):
        micro = lax.rem(section[0] + TICKS - tick, TICKS)
        stamp = steps[micro] + (micro > section[0]).astype(jnp.int32)
        copies.append(
            pltpu.make_async_copy(table.at[stamp], rows.at[pl.ds(3 * tick, 3)], sem.at[TICKS + tick])
        )
    copies.append(pltpu.make_async_copy(query_gain, rows.at[3 * TICKS], sem.at[2 * TICKS]))
    copies.append(pltpu.make_async_copy(key_gain, rows.at[3 * TICKS + 1], sem.at[2 * TICKS + 1]))
    for copy in copies:
        copy.start()
    for copy in copies:
        copy.wait()
    width = entering.shape[1]
    for place in (out, out_mods):
        place[0:6, 0:width] = stale[:, 0]
        place[6:8, 0:width] = entering[...]
        place[0:6, width:CHUNK] = stale[:, 1, 0 : 3 * PIECE]
        for pair in range(3):
            place[6:8, width + pair * PIECE : width + (pair + 1) * PIECE] = stale[
                2 * pair : 2 * pair + 2, 1, 3 * PIECE :
            ]
    upper = jnp.concatenate([rows[index] for index in range(8)], axis=0)
    lower = [rows[index] for index in range(8, 14)]
    split = 3 * PIECE
    first = jnp.concatenate([row[:, 0:split] for row in lower], axis=0)
    last = [
        jnp.concatenate([lower[2 * pair][:, split:], lower[2 * pair + 1][:, split:]], axis=0)
        for pair in range(3)
    ]
    lower = jnp.concatenate([first, jnp.concatenate(last, axis=1)], axis=0)
    whole = jnp.concatenate([upper, lower], axis=1)
    high = whole.astype(out.dtype)
    out_mods[:, CHUNK : 2 * CHUNK] = high
    out_mods[:, 2 * CHUNK :] = (whole - high.astype(jnp.float32)).astype(out.dtype)


def keep_mods(mods, layer, chunk):
    both = chunk[:, CHUNK : 2 * CHUNK].astype(jnp.float32) + chunk[:, 2 * CHUNK :].astype(jnp.float32)
    width = mods.shape[2]
    mods[layer, 0:8] = both[:, 0:width]
    mods[layer, 8:14, 0 : 3 * PIECE] = both[0:6, width:]
    for pair in range(3):
        begin = width + pair * PIECE
        mods[layer, 8 + 2 * pair : 10 + 2 * pair, 3 * PIECE :] = both[6:8, begin : begin + PIECE]


def near_kernel(own, other, keys, values, states, mods, placed):
    for place in placed:
        clear_placed(*place)
    keep_mods(mods, 0, own[0])
    keep_mods(mods, 1, other[0])
    fill(((0, own), (1, other)), keys, values, states)
    states[0], states[1] = steps(
        [
            (states[0].astype(jnp.float32), mods.at[0], 0, 0, placed[0]),
            (states[1].astype(jnp.float32), mods.at[1], 1, 0, placed[1]),
        ],
        keys,
        values,
    )


def far_kernel(
    section,
    far,
    across,
    near_keys,
    near_values,
    near_states,
    near_mods,
    hidden,
    cache,
    keys,
    values,
    mods,
    states,
    placed,
    sem,
):
    beside = jnp.where(section[0] % 2 == 0, 1, TICKS - 1)
    cross = TICKS - beside
    copies = [
        pltpu.make_async_copy(near_keys.at[1], keys.at[beside], sem.at[0]),
        pltpu.make_async_copy(near_values.at[1], values.at[beside], sem.at[1]),
    ]
    for copy in copies:
        copy.start()
    for place in placed:
        clear_placed(*place)
    mods[0] = near_mods[0]
    mods[beside] = near_mods[1]
    keep_mods(mods, 2, far[0])
    keep_mods(mods, cross, across[0])
    fill(((2, far), (cross, across)), keys, values, states)
    states[0] = near_states[0]
    states[beside] = near_states[1]

    def rows(micro):
        return states[micro].astype(jnp.float32)

    states[2], states[cross] = steps(
        [
            (rows(2), mods.at[2], 2, 0, placed[0]),
            (rows(cross), mods.at[cross], cross, 0, placed[1]),
        ],
        keys,
        values,
    )
    for copy in copies:
        copy.wait()
    for tick in range(1, TICKS):
        group = [
            (rows(micro), mods.at[micro + tick], micro + tick, tick, placed[micro])
            for micro in range(TICKS - tick)
        ]
        group.append((rows(TICKS - tick), mods.at[0], 0, tick, None))
        for micro, result in enumerate(steps(group, keys, values)):
            states[micro] = result
    hidden[...] = states[0, 0:2]
    for tick in range(TICKS):
        start = STALE + tick * ROWS
        micro = lax.rem(section[0] + TICKS - tick, TICKS)
        pairs = ((near_keys, near_values), (keys, values))[tick > 0]
        for part, source in enumerate(pairs):
            made = source[0, start : start + ROWS]
            for row in range(2):
                cache[micro * 2 + row, part : part + 1] = made[row : row + 1]


VMEM = pl.BlockSpec(memory_space=pltpu.VMEM)
SMEM = pl.BlockSpec(memory_space=pltpu.SMEM)
HBM = pl.BlockSpec(memory_space=pltpu.HBM)


def call(kernel, out_shape, in_specs, scratch=(), limit=12 << 20):
    return pl.pallas_call(
        kernel,
        out_shape=out_shape,
        in_specs=in_specs,
        out_specs=jax.tree.map(lambda _: VMEM, out_shape),
        scratch_shapes=list(scratch),
        compiler_params=pltpu.CompilerParams(vmem_limit_bytes=limit),
    )


def fast_shards(*arrays):
    return fast_body(*arrays)


def fast_body(hidden, kv_cache, step_index, mod_table, query_gain, key_gain):
    width = hidden.shape[-1]
    section_now = lax.axis_index("section")
    section = section_now.reshape(1).astype(jnp.int32)
    shape = jax.ShapeDtypeStruct
    bf16 = jnp.bfloat16

    pack, with_mods = call(
        load_kernel,
        (shape((8, CHUNK), bf16), shape((8, 3 * CHUNK), bf16)),
        [SMEM, SMEM] + [HBM] * 5,
        [
            pltpu.VMEM((6, 2, width), bf16),
            pltpu.VMEM((2, width), bf16),
            pltpu.VMEM((3 * TICKS + 2, 1, width), jnp.float32),
            pltpu.SemaphoreType.DMA((2 * TICKS + 2,)),
        ],
        60 << 20,
    )(section, step_index, kv_cache, hidden, mod_table.reshape(-1, 3, 1, width), query_gain, key_gain)
    own = [with_mods] + [swap(pack, "patch", bit) for bit in (1, 2, 3)]
    other = [swap(chunk, "section", 1) for chunk in own]
    far = [swap(chunk, "section", 2) for chunk in own]
    across = [swap(chunk, "section", 1) for chunk in far]

    def near(*refs):
        near_kernel(refs[0:4], refs[4:8], *refs[8:12], (refs[12:15], refs[15:18]))

    def distant(section_ref, *refs):
        places = (refs[18:21], refs[21:24], refs[24:27])
        far_kernel(section_ref, refs[0:4], refs[4:8], *refs[8:18], places, refs[27])

    def layers(count):
        return shape((count, SLOTS, width), bf16)

    def states(count):
        return shape((count, ROWS, width), bf16)

    placed = [
        pltpu.VMEM(((end - begin) * ROWS, (end - begin) * HEAD), bf16) for begin, end in GROUPS
    ]
    keys, values, after, mods = call(
        near,
        (layers(2), layers(2), states(2), shape((2, 16, width), jnp.float32)),
        [VMEM] * 8,
        placed * 2,
    )(*own, *other)
    ended, cache = call(
        distant,
        (shape((2, width), bf16), shape((2 * TICKS, 2, width), bf16)),
        [SMEM] + [VMEM] * 12,
        [
            pltpu.VMEM((TICKS, SLOTS, width), bf16),
            pltpu.VMEM((TICKS, SLOTS, width), bf16),
            pltpu.VMEM((TICKS, 16, width), jnp.float32),
            pltpu.VMEM((TICKS, ROWS, width), bf16),
        ]
        + placed * 3
        + [pltpu.SemaphoreType.DMA((2,))],
    )(section, *far, *across, keys, values, after, mods)
    return ended[None], cache[None]


def solution(mesh):
    in_specs = (
        P("section", "patch", None),
        P("section", ("group", "patch"), None, None),
        P("group"),
        P(None, "section", None, None),
        P("section", None),
        P("section", None),
    )
    out_specs = (
        P("section", ("group", "patch"), None),
        P("section", ("group", "patch"), None, None),
    )
    fits = mesh.shape["section"] == TICKS and mesh.shape["patch"] == 4
    shards = fast_shards if fits else general_shards
    return jax.shard_map(shards, mesh=mesh, in_specs=in_specs, out_specs=out_specs, check_vma=False)
```

```python
import jax
import jax.numpy as jnp
from jax import lax
from jax.experimental import pallas as pl
from jax.experimental.pallas import tpu as pltpu
from jax.sharding import PartitionSpec as P

HEAD = 128
HEADS = 20
TICKS = 4
ROWS = 8
STALE = 32
SLOTS = STALE + TICKS * ROWS
PIECE = 640
CHUNK = 7 * PIECE


def from_behind(value, axis, steps):
    count = lax.axis_size(axis)
    pairs = [(source, (source + steps) % count) for source in range(count)]
    return lax.ppermute(value, axis, pairs)


def modulate(rows_in, shift_row, scale_row):
    average = jnp.mean(rows_in, axis=-1, keepdims=True)
    centred = rows_in - average
    variance = jnp.mean(centred * centred, axis=-1, keepdims=True)
    return centred / jnp.sqrt(variance + 1e-06) * (1.0 + scale_row) + shift_row


def head_norm(rows_in):
    shaped = rows_in.reshape(rows_in.shape[0], HEADS, HEAD)
    square = jnp.mean(shaped * shaped, axis=-1, keepdims=True)
    return (shaped / jnp.sqrt(square + 1e-06)).reshape(rows_in.shape)


def attend(queries, keys_all, values_all):
    count = queries.shape[0]
    query_heads = queries.reshape(count, HEADS, HEAD)
    key_heads = keys_all.reshape(-1, HEADS, HEAD)
    value_heads = values_all.reshape(-1, HEADS, HEAD)
    scores = jnp.einsum(
        "rhd,khd->rhk", query_heads, key_heads, preferred_element_type=jnp.float32
    ) * HEAD ** (-0.5)
    highest = jnp.max(scores, axis=-1)
    weights = jnp.exp(scores - highest[:, :, None]).astype(jnp.bfloat16)
    totals = jnp.sum(weights.astype(jnp.float32), axis=-1)
    summed = jnp.einsum("rhk,khd->rhd", weights, value_heads, preferred_element_type=jnp.float32)
    return (summed / totals[:, :, None]).reshape(count, HEADS * HEAD)


def general_shards(hidden, kv_cache, step_index, mod_table, query_gain, key_gain):
    sections = lax.axis_size("section")
    patches = lax.axis_size("patch")
    section_now = lax.axis_index("section")
    state = hidden[0]
    rows = state.shape[0]
    width = state.shape[1]
    own_cache = kv_cache[0].reshape(sections, rows, 2, width)
    table = mod_table[:, 0]
    whole = lax.all_gather(kv_cache[0], "patch", axis=0, tiled=True).reshape(
        patches, sections, rows, 2, width
    )
    for tick_num in range(TICKS):
        micro = (section_now - tick_num) % sections
        wraps = (micro + tick_num) // sections
        stamp = jnp.sum(jnp.where(jnp.arange(sections) == micro, step_index, 0)) + wraps
        chooser = (jnp.arange(table.shape[0]) == stamp)[:, None, None]
        picked = jnp.sum(jnp.where(chooser, table, 0.0), axis=0)
        modulated = modulate(state.astype(jnp.float32), picked[0], picked[1])
        normed = head_norm(modulated)
        queries = (normed * query_gain[0]).astype(jnp.bfloat16)
        keys_now = (normed * key_gain[0]).astype(jnp.bfloat16)
        fresh = jnp.stack([keys_now, modulated.astype(jnp.bfloat16)], axis=1)
        own_cache = lax.dynamic_update_slice_in_dim(own_cache, fresh[None], micro, 0)
        fresh_all = lax.all_gather(fresh, "patch", axis=0, tiled=True).reshape(
            patches, 1, rows, 2, width
        )
        whole = lax.dynamic_update_slice_in_dim(whole, fresh_all, micro, 1)
        flat = whole.reshape(-1, 2, width)
        attended = attend(queries, flat[:, 0], flat[:, 1])
        updated = (state.astype(jnp.float32) + picked[2] * attended).astype(jnp.bfloat16)
        state = from_behind(updated, "section", 1)
    return (state[None], own_cache.reshape(kv_cache.shape))


def swap(value, axis, bit):
    count = lax.axis_size(axis)
    return lax.ppermute(value, axis, [(source, source ^ bit) for source in range(count)])


def mod_row(mods, index):
    return mods[pl.ds(index, ROWS, stride=0), :]


def project(rows_in, mods, tick):
    shift_row = mod_row(mods, 3 * tick)
    scale_row = mod_row(mods, 3 * tick + 1)
    average = jnp.mean(rows_in, axis=-1, keepdims=True)
    centred = rows_in - average
    variance = jnp.mean(centred * centred, axis=-1, keepdims=True)
    modulated = centred * lax.rsqrt(variance + 1e-06) * (1.0 + scale_row) + shift_row
    normed = []
    for head in range(HEADS):
        part = modulated[:, head * HEAD : (head + 1) * HEAD]
        square = jnp.mean(part * part, axis=-1, keepdims=True)
        normed.append(part * lax.rsqrt(square + 1e-06))
    return modulated, jnp.concatenate(normed, axis=1)


GROUPS = ((0, 8), (8, 16), (16, 20))


def clear_placed(*placed):
    for place in placed:
        place[...] = jnp.zeros_like(place)


def weigh(scores, tick):
    key = lax.broadcasted_iota(jnp.int32, scores.shape, 0)
    stale = (key < STALE) & (key % 8 < 2 * (TICKS - 1 - tick))
    fresh = (key >= STALE) & (key < STALE + (tick + 1) * ROWS)
    scores = jnp.where(stale | fresh, scores, -3.0e38)
    highest = jnp.max(scores, axis=0, keepdims=True)
    weights = jnp.exp((scores - highest) * HEAD ** (-0.5))
    return weights.T.astype(jnp.bfloat16)


def steps(group, keys, values):
    made = []
    for rows_in, mods, layer, tick, placed in group:
        modulated, normed = project(rows_in, mods, tick)
        slot = slice(STALE + tick * ROWS, STALE + (tick + 1) * ROWS)
        keys[layer, slot] = (normed * mod_row(mods, 3 * TICKS + 1)).astype(jnp.bfloat16)
        values[layer, slot] = modulated.astype(jnp.bfloat16)
        if placed is not None:
            made.append((normed * mod_row(mods, 3 * TICKS)).astype(jnp.bfloat16))
    group = [entry for entry in group if entry[4] is not None]
    for queries, (_, _, _, _, placed) in zip(made, group):
        for place, (begin, end) in zip(placed, GROUPS):
            for head in range(begin, end):
                low = head - begin
                place[low * ROWS : (low + 1) * ROWS, low * HEAD : (low + 1) * HEAD] = queries[
                    :, head * HEAD : (head + 1) * HEAD
                ]
    against = (((1,), (1,)), ((), ()))
    scores = [
        [
            lax.dot_general(
                keys[layer, :, begin * HEAD : end * HEAD],
                place[...],
                against,
                preferred_element_type=jnp.float32,
            )
            for place, (begin, end) in zip(placed, GROUPS)
        ]
        for _, _, layer, _, placed in group
    ]
    weights = [
        [weigh(part, entry[3]) for part in parts] for parts, entry in zip(scores, group)
    ]
    ones = jnp.ones((SLOTS, HEAD), jnp.bfloat16)
    results = []
    for chosen, (rows_in, mods, layer, tick, _) in zip(weights, group):
        parts = []
        for part, (begin, end) in zip(chosen, GROUPS):
            totals = jnp.dot(part, ones, preferred_element_type=jnp.float32)
            for head in range(begin, end, 2):
                low = (head - begin) * ROWS
                summed = jnp.dot(
                    part[low : low + 2 * ROWS],
                    values[layer, :, head * HEAD : (head + 2) * HEAD],
                    preferred_element_type=jnp.float32,
                )
                parts.append(summed[0:ROWS, 0:HEAD] / totals[low : low + ROWS])
                parts.append(summed[ROWS:, HEAD:] / totals[low + ROWS : low + 2 * ROWS])
        attended = jnp.concatenate(parts, axis=1)
        results.append((rows_in + mod_row(mods, 3 * tick + 2) * attended).astype(jnp.bfloat16))
    return results


def fill(entries, keys, values, states):
    width = keys.shape[2]
    pieces = width // PIECE

    @pl.loop(0, pieces)
    def _(index):
        span = pl.ds(pl.multiple_of(index * PIECE, PIECE), PIECE)
        beside = pl.ds(pl.multiple_of(width + jnp.minimum(index, pieces - 2) * PIECE, PIECE), PIECE)
        for layer, number, chunk in entries:
            keys[layer, number * 8 : number * 8 + 8, span] = chunk[:, span]
            values[layer, number * 8 : number * 8 + 8, span] = chunk[:, beside]
            states[layer, number * 2 : number * 2 + 2, span] = chunk[6:8, span].astype(jnp.float32)

    last = width - PIECE
    for layer, number, chunk in entries:
        for pair in range(3):
            low = number * 8 + 2 * pair
            beside = width + pair * PIECE
            values[layer, low : low + 2, last:] = chunk[6:8, beside : beside + PIECE]


def load_kernel(
    section, steps, cache, hidden, table, query_gain, key_gain, out, out_mods, stale, entering, rows, sem
):
    copies = [pltpu.make_async_copy(hidden.at[0], entering, sem.at[0])]
    for later in range(1, TICKS):
        micro = lax.rem(section[0] + later, TICKS)
        copies.append(
            pltpu.make_async_copy(
                cache.at[0, pl.ds(2 * micro, 2)], stale.at[pl.ds(2 * later - 2, 2)], sem.at[later]
            )
        )
    for tick in range(TICKS):
        micro = lax.rem(section[0] + TICKS - tick, TICKS)
        stamp = steps[micro] + (micro > section[0]).astype(jnp.int32)
        copies.append(
            pltpu.make_async_copy(table.at[stamp], rows.at[pl.ds(3 * tick, 3)], sem.at[TICKS + tick])
        )
    copies.append(pltpu.make_async_copy(query_gain, rows.at[3 * TICKS], sem.at[2 * TICKS]))
    copies.append(pltpu.make_async_copy(key_gain, rows.at[3 * TICKS + 1], sem.at[2 * TICKS + 1]))
    for copy in copies:
        copy.start()
    for copy in copies:
        copy.wait()
    width = entering.shape[1]
    out[0:6, 0:width] = stale[:, 0]
    out[6:8, 0:width] = entering[...]
    out[0:6, width:] = stale[:, 1, 0 : 3 * PIECE]
    for pair in range(3):
        out[6:8, width + pair * PIECE : width + (pair + 1) * PIECE] = stale[
            2 * pair : 2 * pair + 2, 1, 3 * PIECE :
        ]
    out_mods[:, 0:CHUNK] = out[...]
    upper = jnp.concatenate([rows[index] for index in range(8)], axis=0)
    lower = [rows[index] for index in range(8, 14)]
    split = 3 * PIECE
    first = jnp.concatenate([row[:, 0:split] for row in lower], axis=0)
    last = [
        jnp.concatenate([lower[2 * pair][:, split:], lower[2 * pair + 1][:, split:]], axis=0)
        for pair in range(3)
    ]
    lower = jnp.concatenate([first, jnp.concatenate(last, axis=1)], axis=0)
    whole = jnp.concatenate([upper, lower], axis=1)
    high = whole.astype(out.dtype)
    out_mods[:, CHUNK : 2 * CHUNK] = high
    out_mods[:, 2 * CHUNK :] = (whole - high.astype(jnp.float32)).astype(out.dtype)


def keep_mods(mods, layer, chunk):
    both = chunk[:, CHUNK : 2 * CHUNK].astype(jnp.float32) + chunk[:, 2 * CHUNK :].astype(jnp.float32)
    width = mods.shape[2]
    mods[layer, 0:8] = both[:, 0:width]
    mods[layer, 8:14, 0 : 3 * PIECE] = both[0:6, width:]
    for pair in range(3):
        begin = width + pair * PIECE
        mods[layer, 8 + 2 * pair : 10 + 2 * pair, 3 * PIECE :] = both[6:8, begin : begin + PIECE]


def stage_kernel(loaded, chunk, mods):
    chunk[...] = loaded[:, 0:CHUNK]
    keep_mods(mods, 0, loaded)


def beside_of(section):
    return jnp.where(section[0] % 2 == 0, 1, TICKS - 1)


def places(placed, number):
    return [place.at[number] for place in placed]


def early_kernel(section, own, other, own_mods, keys, values, states, mods, *placed):
    beside = beside_of(section)
    clear_placed(*placed)
    values[:, STALE:] = jnp.zeros((TICKS, SLOTS - STALE, values.shape[2]), values.dtype)
    mods[0] = own_mods[0]
    keep_mods(mods, beside, other[0])
    fill(
        [(0, number, chunk) for number, chunk in enumerate(own)]
        + [(beside, number, chunk) for number, chunk in enumerate(other)],
        keys,
        values,
        states,
    )


def near_kernel(section, late, keys, values, states, mods, *placed):
    beside = beside_of(section)
    fill([(beside, 3, late)], keys, values, states)
    results = steps(
        [
            (states[0], mods.at[0], 0, 0, places(placed, 0)),
            (states[beside], mods.at[beside], beside, 0, places(placed, 1)),
        ],
        keys,
        values,
    )
    states[0] = results[0].astype(jnp.float32)
    states[beside] = results[1].astype(jnp.float32)


def late_kernel(section, far, across, keys, values, states, mods, *placed):
    cross = TICKS - beside_of(section)
    keep_mods(mods, 2, far[0])
    keep_mods(mods, cross, across[0])
    fill(
        [(2, number, chunk) for number, chunk in enumerate(far)]
        + [(cross, number, chunk) for number, chunk in enumerate(across)],
        keys,
        values,
        states,
    )


def far_kernel(section, late, keys, values, states, mods, placed, hidden, cache):
    cross = TICKS - beside_of(section)
    fill([(cross, 3, late)], keys, values, states)
    results = steps(
        [
            (states[2], mods.at[2], 2, 0, places(placed, 0)),
            (states[cross], mods.at[cross], cross, 0, places(placed, 1)),
        ],
        keys,
        values,
    )
    states[2] = results[0].astype(jnp.float32)
    states[cross] = results[1].astype(jnp.float32)
    for tick in range(1, TICKS):
        group = [
            (states[micro], mods.at[micro + tick], micro + tick, tick, places(placed, micro))
            for micro in range(TICKS - tick)
        ]
        group.append((states[TICKS - tick], mods.at[0], 0, tick, None))
        results = steps(group, keys, values)
        for micro, result in enumerate(results):
            states[micro] = result.astype(jnp.float32)
    hidden[...] = results[0][0:2]
    for tick in range(TICKS):
        start = STALE + tick * ROWS
        micro = lax.rem(section[0] + TICKS - tick, TICKS)
        for part, source in enumerate((keys, values)):
            made = source[0, start : start + ROWS]
            for row in range(2):
                cache[micro * 2 + row, part : part + 1] = made[row : row + 1]


VMEM = pl.BlockSpec(memory_space=pltpu.VMEM)
SMEM = pl.BlockSpec(memory_space=pltpu.SMEM)
HBM = pl.BlockSpec(memory_space=pltpu.HBM)


def call(kernel, out_shape, in_specs, scratch=(), limit=12 << 20, aliases=None):
    return pl.pallas_call(
        kernel,
        out_shape=out_shape,
        in_specs=in_specs,
        out_specs=jax.tree.map(lambda _: VMEM, out_shape),
        scratch_shapes=list(scratch),
        input_output_aliases=aliases or {},
        compiler_params=pltpu.CompilerParams(vmem_limit_bytes=limit),
    )


def fast_shards(*arrays):
    return fast_body(*arrays)


def fast_body(hidden, kv_cache, step_index, mod_table, query_gain, key_gain):
    width = hidden.shape[-1]
    section_now = lax.axis_index("section")
    section = section_now.reshape(1).astype(jnp.int32)
    shape = jax.ShapeDtypeStruct
    bf16 = jnp.bfloat16

    pack, with_mods = call(
        load_kernel,
        (shape((8, CHUNK), bf16), shape((8, 3 * CHUNK), bf16)),
        [SMEM, SMEM] + [HBM] * 5,
        [
            pltpu.VMEM((6, 2, width), bf16),
            pltpu.VMEM((2, width), bf16),
            pltpu.VMEM((3 * TICKS + 2, 1, width), jnp.float32),
            pltpu.SemaphoreType.DMA((2 * TICKS + 2,)),
        ],
        60 << 20,
    )(section, step_index, kv_cache, hidden, mod_table.reshape(-1, 3, 1, width), query_gain, key_gain)
    own = [with_mods] + [swap(pack, "patch", bit) for bit in (1, 2, 3)]
    other = [swap(chunk, "section", 1) for chunk in own]
    far = [swap(chunk, "section", 2) for chunk in own]
    across = [swap(chunk, "section", 1) for chunk in far]

    staged, staged_mods = call(
        stage_kernel, (shape((8, CHUNK), bf16), shape((1, 16, width), jnp.float32)), [VMEM]
    )(with_mods)

    kept = (
        shape((TICKS, SLOTS, width), bf16),
        shape((TICKS, SLOTS, width), bf16),
        shape((TICKS, ROWS, width), jnp.float32),
        shape((TICKS, 16, width), jnp.float32),
    ) + tuple(shape((3, (end - begin) * ROWS, (end - begin) * HEAD), bf16) for begin, end in GROUPS)
    count = len(kept)

    def early(section_ref, *refs):
        early_kernel(section_ref, refs[0:4], refs[4:7], *refs[7:])

    def near(*refs):
        near_kernel(*refs[0:2], *refs[2 + count :])

    def late(section_ref, *refs):
        late_kernel(section_ref, refs[0:4], refs[4:7], *refs[7 + count :])

    def distant(*refs):
        held = refs[2 + count : 2 + 2 * count]
        far_kernel(*refs[0:2], *held[0:4], held[4:], *refs[2 + 2 * count :])

    def passed(kernel, inputs, buffers, extra=()):
        first = 1 + len(inputs)
        return call(
            kernel,
            kept + tuple(extra),
            [SMEM] + [VMEM] * (len(inputs) + len(buffers)),
            aliases={first + index: index for index in range(len(buffers))},
        )(section, *inputs, *buffers)

    buffers = passed(early, (staged, *own[1:], *other[0:3], staged_mods), ())
    buffers = passed(near, (other[3],), buffers)
    buffers = passed(late, (*far, *across[0:3]), buffers)
    ended, cache = passed(
        distant,
        (across[3],),
        buffers,
        (shape((2, width), bf16), shape((2 * TICKS, 2, width), bf16)),
    )[count:]
    return ended[None], cache[None]


def solution(mesh):
    in_specs = (
        P("section", "patch", None),
        P("section", ("group", "patch"), None, None),
        P("group"),
        P(None, "section", None, None),
        P("section", None),
        P("section", None),
    )
    out_specs = (
        P("section", ("group", "patch"), None),
        P("section", ("group", "patch"), None, None),
    )
    fits = mesh.shape["section"] == TICKS and mesh.shape["patch"] == 4
    shards = fast_shards if fits else general_shards
    return jax.shard_map(shards, mesh=mesh, in_specs=in_specs, out_specs=out_specs, check_vma=False)
```

```python
import jax
import jax.numpy as jnp
from jax import lax
from jax.experimental import pallas as pl
from jax.experimental.pallas import tpu as pltpu
from jax.sharding import PartitionSpec as P

HEAD = 128
HEADS = 20
TICKS = 4
ROWS = 8
STALE = 32
SLOTS = STALE + TICKS * ROWS
PIECE = 640
CHUNK = 7 * PIECE


def from_behind(value, axis, steps):
    count = lax.axis_size(axis)
    pairs = [(source, (source + steps) % count) for source in range(count)]
    return lax.ppermute(value, axis, pairs)


def modulate(rows_in, shift_row, scale_row):
    average = jnp.mean(rows_in, axis=-1, keepdims=True)
    centred = rows_in - average
    variance = jnp.mean(centred * centred, axis=-1, keepdims=True)
    return centred / jnp.sqrt(variance + 1e-06) * (1.0 + scale_row) + shift_row


def head_norm(rows_in):
    shaped = rows_in.reshape(rows_in.shape[0], HEADS, HEAD)
    square = jnp.mean(shaped * shaped, axis=-1, keepdims=True)
    return (shaped / jnp.sqrt(square + 1e-06)).reshape(rows_in.shape)


def attend(queries, keys_all, values_all):
    count = queries.shape[0]
    query_heads = queries.reshape(count, HEADS, HEAD)
    key_heads = keys_all.reshape(-1, HEADS, HEAD)
    value_heads = values_all.reshape(-1, HEADS, HEAD)
    scores = jnp.einsum(
        "rhd,khd->rhk", query_heads, key_heads, preferred_element_type=jnp.float32
    ) * HEAD ** (-0.5)
    highest = jnp.max(scores, axis=-1)
    weights = jnp.exp(scores - highest[:, :, None]).astype(jnp.bfloat16)
    totals = jnp.sum(weights.astype(jnp.float32), axis=-1)
    summed = jnp.einsum("rhk,khd->rhd", weights, value_heads, preferred_element_type=jnp.float32)
    return (summed / totals[:, :, None]).reshape(count, HEADS * HEAD)


def general_shards(hidden, kv_cache, step_index, mod_table, query_gain, key_gain):
    sections = lax.axis_size("section")
    patches = lax.axis_size("patch")
    section_now = lax.axis_index("section")
    state = hidden[0]
    rows = state.shape[0]
    width = state.shape[1]
    own_cache = kv_cache[0].reshape(sections, rows, 2, width)
    table = mod_table[:, 0]
    whole = lax.all_gather(kv_cache[0], "patch", axis=0, tiled=True).reshape(
        patches, sections, rows, 2, width
    )
    for tick_num in range(TICKS):
        micro = (section_now - tick_num) % sections
        wraps = (micro + tick_num) // sections
        stamp = jnp.sum(jnp.where(jnp.arange(sections) == micro, step_index, 0)) + wraps
        chooser = (jnp.arange(table.shape[0]) == stamp)[:, None, None]
        picked = jnp.sum(jnp.where(chooser, table, 0.0), axis=0)
        modulated = modulate(state.astype(jnp.float32), picked[0], picked[1])
        normed = head_norm(modulated)
        queries = (normed * query_gain[0]).astype(jnp.bfloat16)
        keys_now = (normed * key_gain[0]).astype(jnp.bfloat16)
        fresh = jnp.stack([keys_now, modulated.astype(jnp.bfloat16)], axis=1)
        own_cache = lax.dynamic_update_slice_in_dim(own_cache, fresh[None], micro, 0)
        fresh_all = lax.all_gather(fresh, "patch", axis=0, tiled=True).reshape(
            patches, 1, rows, 2, width
        )
        whole = lax.dynamic_update_slice_in_dim(whole, fresh_all, micro, 1)
        flat = whole.reshape(-1, 2, width)
        attended = attend(queries, flat[:, 0], flat[:, 1])
        updated = (state.astype(jnp.float32) + picked[2] * attended).astype(jnp.bfloat16)
        state = from_behind(updated, "section", 1)
    return (state[None], own_cache.reshape(kv_cache.shape))


def swap(value, axis, bit):
    count = lax.axis_size(axis)
    return lax.ppermute(value, axis, [(source, source ^ bit) for source in range(count)])


def mod_row(mods, index):
    return mods[pl.ds(index, ROWS, stride=0), :]


def project(rows_in, shift_row, scale_row):
    average = jnp.mean(rows_in, axis=-1, keepdims=True)
    centred = rows_in - average
    variance = jnp.mean(centred * centred, axis=-1, keepdims=True)
    modulated = centred * lax.rsqrt(variance + 1e-06) * (1.0 + scale_row) + shift_row
    normed = []
    for head in range(HEADS):
        part = modulated[:, head * HEAD : (head + 1) * HEAD]
        square = jnp.mean(part * part, axis=-1, keepdims=True)
        normed.append(part * lax.rsqrt(square + 1e-06))
    return modulated, jnp.concatenate(normed, axis=1)


GROUPS = ((0, 10), (10, 20))


def clear_placed(*placed):
    for place in placed:
        place[...] = jnp.zeros_like(place)


def weigh(scores, tick):
    key = lax.broadcasted_iota(jnp.int32, scores.shape, 0)
    stale = (key < STALE) & (key % 8 < 2 * (TICKS - 1 - tick))
    fresh = (key >= STALE) & (key < STALE + (tick + 1) * ROWS)
    scores = jnp.where(stale | fresh, scores, -3.0e38)
    highest = jnp.max(scores, axis=0, keepdims=True)
    weights = jnp.exp((scores - highest) * HEAD ** (-0.5))
    return weights.T.astype(jnp.bfloat16)


def steps(group, keys, values):
    made = []
    for rows_in, mods, layer, tick, placed in group:
        modulated, normed = project(rows_in, mod_row(mods, 3 * tick), mod_row(mods, 3 * tick + 1))
        slot = slice(STALE + tick * ROWS, STALE + (tick + 1) * ROWS)
        keys[layer, slot] = (normed * mod_row(mods, 3 * TICKS + 1)).astype(jnp.bfloat16)
        values[layer, slot] = modulated.astype(jnp.bfloat16)
        made.append((normed * mod_row(mods, 3 * TICKS)).astype(jnp.bfloat16))
    for queries, (_, _, _, _, placed) in zip(made, group):
        for place, (begin, end) in zip(placed, GROUPS):
            for head in range(begin, end):
                low = head - begin
                place[low * ROWS : (low + 1) * ROWS, low * HEAD : (low + 1) * HEAD] = queries[
                    :, head * HEAD : (head + 1) * HEAD
                ]
    against = (((1,), (1,)), ((), ()))
    scores = [
        [
            lax.dot_general(
                keys[layer, :, begin * HEAD : end * HEAD],
                place[...],
                against,
                preferred_element_type=jnp.float32,
            )
            for place, (begin, end) in zip(placed, GROUPS)
        ]
        for _, _, layer, _, placed in group
    ]
    weights = [
        [weigh(part, entry[3]) for part in parts] for parts, entry in zip(scores, group)
    ]
    ones = jnp.ones((SLOTS, HEAD), jnp.bfloat16)
    results = []
    for chosen, (rows_in, mods, layer, tick, _) in zip(weights, group):
        parts = []
        for part, (begin, end) in zip(chosen, GROUPS):
            totals = jnp.dot(part, ones, preferred_element_type=jnp.float32)
            for head in range(begin, end, 2):
                low = (head - begin) * ROWS
                summed = jnp.dot(
                    part[low : low + 2 * ROWS],
                    values[layer, :, head * HEAD : (head + 2) * HEAD],
                    preferred_element_type=jnp.float32,
                )
                parts.append(summed[0:ROWS, 0:HEAD] / totals[low : low + ROWS])
                parts.append(summed[ROWS:, HEAD:] / totals[low + ROWS : low + 2 * ROWS])
        attended = jnp.concatenate(parts, axis=1)
        results.append((rows_in + mod_row(mods, 3 * tick + 2) * attended).astype(jnp.bfloat16))
    return results


def fill(entries, keys, values, states):
    width = keys.shape[2]
    pieces = width // PIECE

    @pl.loop(0, pieces)
    def _(index):
        span = pl.ds(pl.multiple_of(index * PIECE, PIECE), PIECE)
        beside = pl.ds(pl.multiple_of(width + jnp.minimum(index, pieces - 2) * PIECE, PIECE), PIECE)
        for layer, number, chunk in entries:
            keys[layer, number * 8 : number * 8 + 8, span] = chunk[:, span]
            values[layer, number * 8 : number * 8 + 8, span] = chunk[:, beside]
            states[layer, number * 2 : number * 2 + 2, span] = chunk[6:8, span].astype(jnp.float32)

    last = width - PIECE
    for layer, number, chunk in entries:
        for pair in range(3):
            low = number * 8 + 2 * pair
            beside = width + pair * PIECE
            values[layer, low : low + 2, last:] = chunk[6:8, beside : beside + PIECE]


def load_kernel(
    cache, hidden, steps, table, query_gain, key_gain, out, out_mods, stale, entering, rows, stamps, sem
):
    section = lax.axis_index("section")
    listed = pltpu.make_async_copy(steps, stamps, sem.at[2 * TICKS + 2])
    listed.start()
    copies = []
    for later in range(1, TICKS):
        micro = lax.rem(section + later, TICKS)
        copies.append(
            pltpu.make_async_copy(
                cache.at[0, pl.ds(2 * micro, 2)], stale.at[pl.ds(2 * later - 2, 2)], sem.at[later]
            )
        )
    copies.append(pltpu.make_async_copy(hidden.at[0], entering, sem.at[0]))
    gains = [
        pltpu.make_async_copy(query_gain, rows.at[3 * TICKS], sem.at[2 * TICKS]),
        pltpu.make_async_copy(key_gain, rows.at[3 * TICKS + 1], sem.at[2 * TICKS + 1]),
    ]
    for copy in copies + gains:
        copy.start()
    listed.wait()
    picks = []
    for tick in range(TICKS):
        micro = lax.rem(section + TICKS - tick, TICKS)
        stamp = stamps[micro] + (micro > section).astype(jnp.int32)
        picks.append(
            pltpu.make_async_copy(table.at[stamp], rows.at[pl.ds(3 * tick, 3)], sem.at[TICKS + tick])
        )
    for copy in picks:
        copy.start()
    for copy in copies:
        copy.wait()
    width = entering.shape[1]
    out[0:6, 0:width] = stale[:, 0]
    out[6:8, 0:width] = entering[...]
    out[0:6, width:] = stale[:, 1, 0 : 3 * PIECE]
    for pair in range(3):
        out[6:8, width + pair * PIECE : width + (pair + 1) * PIECE] = stale[
            2 * pair : 2 * pair + 2, 1, 3 * PIECE :
        ]
    out_mods[:, 0:CHUNK] = out[...]
    for copy in gains + picks:
        copy.wait()
    upper = jnp.concatenate([rows[index] for index in range(8)], axis=0)
    lower = [rows[index] for index in range(8, 14)]
    split = 3 * PIECE
    first = jnp.concatenate([row[:, 0:split] for row in lower], axis=0)
    last = [
        jnp.concatenate([lower[2 * pair][:, split:], lower[2 * pair + 1][:, split:]], axis=0)
        for pair in range(3)
    ]
    lower = jnp.concatenate([first, jnp.concatenate(last, axis=1)], axis=0)
    whole = jnp.concatenate([upper, lower], axis=1)
    high = whole.astype(out.dtype)
    out_mods[:, CHUNK : 2 * CHUNK] = high
    out_mods[:, 2 * CHUNK :] = (whole - high.astype(jnp.float32)).astype(out.dtype)


def keep_mods(mods, layer, chunk):
    both = chunk[:, CHUNK : 2 * CHUNK].astype(jnp.float32) + chunk[:, 2 * CHUNK :].astype(jnp.float32)
    width = mods.shape[2]
    mods[layer, 0:8] = both[:, 0:width]
    mods[layer, 8:14, 0 : 3 * PIECE] = both[0:6, width:]
    for pair in range(3):
        begin = width + pair * PIECE
        mods[layer, 8 + 2 * pair : 10 + 2 * pair, 3 * PIECE :] = both[6:8, begin : begin + PIECE]


def stage_kernel(loaded, chunk, mods):
    chunk[...] = loaded[:, 0:CHUNK]
    keep_mods(mods, 0, loaded)


def beside_of(section):
    return jnp.where(section[0] % 2 == 0, 1, TICKS - 1)


def places(placed, number):
    return [place.at[number] for place in placed]


def early_kernel(section, own, other, own_mods, keys, values, states, mods, *placed):
    beside = beside_of(section)
    clear_placed(*placed)
    values[:, STALE:] = jnp.zeros((TICKS, SLOTS - STALE, values.shape[2]), values.dtype)
    mods[0] = own_mods[0]
    keep_mods(mods, beside, other[0])
    fill(
        [(0, number, chunk) for number, chunk in enumerate(own)]
        + [(beside, number, chunk) for number, chunk in enumerate(other)],
        keys,
        values,
        states,
    )


def near_kernel(section, late, keys, values, states, mods, *placed):
    beside = beside_of(section)
    fill([(beside, 3, late)], keys, values, states)
    results = steps(
        [
            (states[0], mods.at[0], 0, 0, places(placed, 0)),
            (states[beside], mods.at[beside], beside, 0, places(placed, 1)),
        ],
        keys,
        values,
    )
    states[0] = results[0].astype(jnp.float32)
    states[beside] = results[1].astype(jnp.float32)


def late_kernel(section, far, across, keys, values, states, mods, *placed):
    cross = TICKS - beside_of(section)
    keep_mods(mods, 2, far[0])
    keep_mods(mods, cross, across[0])
    fill(
        [(2, number, chunk) for number, chunk in enumerate(far)]
        + [(cross, number, chunk) for number, chunk in enumerate(across)],
        keys,
        values,
        states,
    )


def own_slots(section, entered, keys, values, mods, cache):
    rows_in = jnp.concatenate(entered + entered[-1:], axis=0)
    row = lax.broadcasted_iota(jnp.int32, rows_in.shape, 0)

    def by_tick(part):
        first, second, third = (mod_row(mods.at[0], 3 * tick + part) for tick in (1, 2, 3))
        return jnp.where(row < 2, first, jnp.where(row < 4, second, third))

    values_now, normed = project(rows_in, by_tick(0), by_tick(1))
    keys_now = normed * mod_row(mods.at[0], 3 * TICKS + 1)
    slot = slice(STALE, STALE + ROWS)
    zeroth = keys[0, slot].astype(jnp.float32), values[0, slot].astype(jnp.float32)
    for tick in range(TICKS):
        micro = lax.rem(section[0] + TICKS - tick, TICKS)
        made_keys, made_values = zeroth if tick == 0 else (keys_now, values_now)
        low = 0 if tick == 0 else 2 * tick - 2
        for index in range(low, low + 2):
            pair = jnp.concatenate(
                [made_keys[index : index + 1], made_values[index : index + 1]], axis=0
            )
            cache[micro * 2 + index - low] = pair.astype(cache.dtype)


def far_kernel(section, late, keys, values, states, mods, placed, hidden, cache):
    cross = TICKS - beside_of(section)
    fill([(cross, 3, late)], keys, values, states)
    results = steps(
        [
            (states[2], mods.at[2], 2, 0, places(placed, 0)),
            (states[cross], mods.at[cross], cross, 0, places(placed, 1)),
        ],
        keys,
        values,
    )
    states[2] = results[0].astype(jnp.float32)
    states[cross] = results[1].astype(jnp.float32)
    entered = [states[3, 0:2]]
    for tick in range(1, TICKS):
        if tick == TICKS - 1:
            own_slots(section, entered, keys, values, mods, cache)
        group = [
            (states[micro], mods.at[micro + tick], micro + tick, tick, places(placed, micro))
            for micro in range(TICKS - tick)
        ]
        results = steps(group, keys, values)
        for micro, result in enumerate(results):
            states[micro] = result.astype(jnp.float32)
        entered.append(results[-1][0:2].astype(jnp.float32))
    hidden[...] = results[0][0:2]


VMEM = pl.BlockSpec(memory_space=pltpu.VMEM)
SMEM = pl.BlockSpec(memory_space=pltpu.SMEM)
HBM = pl.BlockSpec(memory_space=pltpu.HBM)


def call(kernel, out_shape, in_specs, scratch=(), limit=12 << 20, aliases=None):
    return pl.pallas_call(
        kernel,
        out_shape=out_shape,
        in_specs=in_specs,
        out_specs=jax.tree.map(lambda _: VMEM, out_shape),
        scratch_shapes=list(scratch),
        input_output_aliases=aliases or {},
        compiler_params=pltpu.CompilerParams(vmem_limit_bytes=limit),
    )


def fast_shards(*arrays):
    return fast_body(*arrays)


def fast_body(hidden, kv_cache, step_index, mod_table, query_gain, key_gain):
    width = hidden.shape[-1]
    section_now = lax.axis_index("section")
    section = section_now.reshape(1).astype(jnp.int32)
    shape = jax.ShapeDtypeStruct
    bf16 = jnp.bfloat16

    pack, with_mods = call(
        load_kernel,
        (shape((8, CHUNK), bf16), shape((8, 3 * CHUNK), bf16)),
        [HBM] * 6,
        [
            pltpu.VMEM((6, 2, width), bf16),
            pltpu.VMEM((2, width), bf16),
            pltpu.VMEM((3 * TICKS + 2, 1, width), jnp.float32),
            pltpu.SMEM((TICKS,), jnp.int32),
            pltpu.SemaphoreType.DMA((2 * TICKS + 3,)),
        ],
        60 << 20,
    )(kv_cache, hidden, step_index, mod_table.reshape(-1, 3, 1, width), query_gain, key_gain)
    own = [with_mods] + [swap(pack, "patch", bit) for bit in (1, 2, 3)]
    other = [swap(chunk, "section", 1) for chunk in own]
    far = [swap(chunk, "section", 2) for chunk in own]
    across = [swap(chunk, "section", 1) for chunk in far]

    staged, staged_mods = call(
        stage_kernel, (shape((8, CHUNK), bf16), shape((1, 16, width), jnp.float32)), [VMEM]
    )(with_mods)

    kept = (
        shape((TICKS, SLOTS, width), bf16),
        shape((TICKS, SLOTS, width), bf16),
        shape((TICKS, ROWS, width), jnp.float32),
        shape((TICKS, 16, width), jnp.float32),
    ) + tuple(shape((3, (end - begin) * ROWS, (end - begin) * HEAD), bf16) for begin, end in GROUPS)
    count = len(kept)

    def early(section_ref, *refs):
        early_kernel(section_ref, refs[0:4], refs[4:7], *refs[7:])

    def near(*refs):
        near_kernel(*refs[0:2], *refs[2 + count :])

    def late(section_ref, *refs):
        late_kernel(section_ref, refs[0:4], refs[4:7], *refs[7 + count :])

    def distant(*refs):
        held = refs[2 + count : 2 + 2 * count]
        far_kernel(*refs[0:2], *held[0:4], held[4:], *refs[2 + 2 * count :])

    def passed(kernel, inputs, buffers, extra=()):
        first = 1 + len(inputs)
        return call(
            kernel,
            kept + tuple(extra),
            [SMEM] + [VMEM] * (len(inputs) + len(buffers)),
            aliases={first + index: index for index in range(len(buffers))},
        )(section, *inputs, *buffers)

    buffers = passed(early, (staged, *own[1:], *other[0:3], staged_mods), ())
    buffers = passed(near, (other[3],), buffers)
    buffers = passed(late, (*far, *across[0:3]), buffers)
    ended, cache = passed(
        distant,
        (across[3],),
        buffers,
        (shape((2, width), bf16), shape((2 * TICKS, 2, width), bf16)),
    )[count:]
    return ended[None], cache[None]


def solution(mesh):
    in_specs = (
        P("section", "patch", None),
        P("section", ("group", "patch"), None, None),
        P("group"),
        P(None, "section", None, None),
        P("section", None),
        P("section", None),
    )
    out_specs = (
        P("section", ("group", "patch"), None),
        P("section", ("group", "patch"), None, None),
    )
    fits = mesh.shape["section"] == TICKS and mesh.shape["patch"] == 4
    shards = fast_shards if fits else general_shards
    return jax.shard_map(shards, mesh=mesh, in_specs=in_specs, out_specs=out_specs, check_vma=False)
```
